32 devices in a mesh: dp: 8 (over z, y), seq: 4 (over x, core).
Axes of the slice: x: 2, y: 2, z: 4, core: 2. Of those that a mesh axis runs over, the one named last changes fastest.
Arguments:
- tokens: bfloat16 [8, 512, 1024], P('dp', 'seq'), may hold values from -6 to 6
- cache_keys: bfloat16 [8, 2048, 1024], P('dp', 'seq')
- cache_values: bfloat16 [8, 2048, 1024], P('dp', 'seq'), may hold values from -6 to 6
- qkv_weight: bfloat16 [1024, 3072], P(None, 'seq'), may hold values from -0.1875 to 0.1875
- qkv_bias: float32 [3072], replicated, may hold values from -3 to 3
- out_weight: bfloat16 [1024, 1024], P('seq', 'dp'), may hold values from -0.1875 to 0.1875
- out_bias: float32 [1024], replicated, may hold values from -3 to 3
- norm_gain: float32 [1024], replicated, may hold values from 0.1 to 1.9
- norm_bias: float32 [1024], replicated, may hold values from -3 to 3
- cached_len: int32 [8], replicated, may hold values from 0 to 2048, as said below
- span_len: int32 [8], replicated, may hold values from 1 to 512, as said below
- slot_request: int32 [8], replicated, may hold values from 0 to 7, each once
Outputs:
- normed: bfloat16 [8, 512, 1024], P('dp', 'seq')
The draws below stay inside these ranges and needn't reach their ends.
Inputs may be any that keep to these rules, and one draw needn't show every extreme that they name: `cached_len`: some request has exactly 2048 cached positions. `span_len`: some request has exactly 512 new tokens in use. `slot_request`: each request names one slot.
All inputs are finite; a program needn't handle non-finite values.
Results may differ from the reference program's by a relative error of at most 0.0085.
Values may be sent and summed in bfloat16 or wider, within the bound.
A program may use at most 64 MiB of HBM per device.

```python
import jax
import jax.numpy as jnp
from jax import lax

D = 1024
HEADS = 16
HEAD_DIM = 64
SPAN_DEV = 128
CACHE_DEV = 512
SPAN = 512
CACHE = 2048
REQUESTS = 8
N_SEQ = 4


def draw_cache_keys(key, part):
    shape = (REQUESTS, CACHE, D)
    return jax.random.normal(key, shape, jnp.float32).astype(jnp.bfloat16)


def draw_cached_len(key, part):
    first, second, third = jax.random.split(jax.random.fold_in(key, 11), 3)
    ranking = jax.random.permutation(first, REQUESTS)
    many = max(1, REQUESTS // 8)
    shorter = jax.random.randint(second, (REQUESTS,), 0, max(2, CACHE // 4))
    longer = CACHE - jax.random.randint(third, (REQUESTS,), 0, max(2, CACHE // 16))
    result = jnp.where(ranking < many, longer, shorter)
    return jnp.where(ranking == 0, CACHE, result).astype(jnp.int32)


def draw_span_len(key, part):
    first, second = jax.random.split(jax.random.fold_in(key, 23), 2)
    ranking = jax.random.permutation(first, REQUESTS)
    drawn = jax.random.randint(second, (REQUESTS,), SPAN // 4, SPAN + 1)
    return jnp.where(ranking == 0, SPAN, drawn).astype(jnp.int32)


def levels(stream_key, extent, shards, low, largest):
    factor_of = 1.0
    for axis_at, blocks in shards:
        heights = jax.random.uniform(jax.random.fold_in(jax.random.fold_in(stream_key, 6), axis_at), (blocks,), jnp.float32, low / len(shards), largest / len(shards))
        factor_of = factor_of * jnp.repeat(jnp.exp(heights), extent[axis_at] // blocks).reshape((-1,) + (1,) * (len(extent) - 1 - axis_at))
    return factor_of


def noise(rng, shape, scale, bound, shards=(), dtype=jnp.bfloat16):
    values = jax.random.normal(rng, shape, jnp.float32) * scale
    if len(shards) > 0:
        values = levels(rng, shape, shards, -0.22, 0.18) * values
    return jnp.clip(values, min=-bound, max=bound).astype(dtype)


def setup_inputs(seed: int = 0) -> dict:
    splits = jax.random.split(jax.random.key(seed), 13)
    return {
        "tokens": noise(splits[0], (REQUESTS, SPAN, D), 1.0, 6.0, ((0, 8), (1, 4))),
        "cache_keys": draw_cache_keys(jax.random.fold_in(splits[12], 71), 0),
        "cache_values": noise(splits[2], (REQUESTS, CACHE, D), 1.0, 6.0, ((0, 8), (1, 4))),
        "qkv_weight": noise(splits[3], (D, 3 * D), D ** -0.5, 0.1875, ((1, 4),)),
        "qkv_bias": noise(splits[4], (3 * D,), 0.5, 3.0, (), jnp.float32),
        "out_weight": noise(splits[5], (D, D), D ** -0.5, 0.1875, ((0, 4), (1, 8))),
        "out_bias": noise(splits[6], (D,), 0.5, 3.0, (), jnp.float32),
        "norm_gain": jnp.clip(1.0 + 0.18 * jax.random.normal(splits[7], (D,), jnp.float32), 0.1, 1.9),
        "norm_bias": noise(splits[8], (D,), 0.5, 3.0, (), jnp.float32),
        "cached_len": draw_cached_len(jax.random.fold_in(splits[12], 71), 0),
        "span_len": draw_span_len(jax.random.fold_in(splits[12], 71), 0),
        "slot_request": jax.random.permutation(splits[11], REQUESTS).astype(jnp.int32),
    }


neg_big = -1e+30

def reference(tokens, cache_keys, cache_values, qkv_weight, qkv_bias, out_weight, out_bias, norm_gain, norm_bias, cached_len, span_len, slot_request):
    scale = HEAD_DIM ** (-0.5)

    def one_slot(index):
        request = slot_request[index]
        cached = cached_len[request]
        filled = span_len[request]
        inputs = tokens[index]
        projected = (jnp.dot(inputs, qkv_weight, preferred_element_type=jnp.float32) + qkv_bias).astype(jnp.bfloat16)
        projected = projected.reshape(SPAN, HEADS, 3, HEAD_DIM)
        queries = projected[:, :, 0]
        new_keys = projected[:, :, 1]
        new_values = projected[:, :, 2]
        keys_all = cache_keys[index].reshape(CACHE, HEADS, HEAD_DIM)
        values_all = cache_values[index].reshape(CACHE, HEADS, HEAD_DIM)
        positions = jnp.arange(SPAN)
        parts = []
        for group in range(N_SEQ):
            keys = jnp.concatenate([keys_all[group * CACHE_DEV:(group + 1) * CACHE_DEV], new_keys[group * SPAN_DEV:(group + 1) * SPAN_DEV]], 0)
            values = jnp.concatenate([values_all[group * CACHE_DEV:(group + 1) * CACHE_DEV], new_values[group * SPAN_DEV:(group + 1) * SPAN_DEV]], 0)
            cache_pos = group * CACHE_DEV + jnp.arange(CACHE_DEV)
            new_pos = group * SPAN_DEV + jnp.arange(SPAN_DEV)
            live_cache = jnp.broadcast_to(cache_pos[None, :] < cached, (SPAN, CACHE_DEV))
            live_new = (new_pos[None, :] <= positions[:, None]) & (new_pos[None, :] < filled)
            live = jnp.concatenate([live_cache, live_new], 1)
            scores = jnp.einsum('thd,khd->htk', queries.astype(jnp.float32), keys.astype(jnp.float32)) * scale
            masked = jnp.where(live[None], scores, neg_big)
            top = lax.optimization_barrier(jnp.max(masked, axis=2))
            weights = jnp.where(live[None], jnp.exp(masked - top[:, :, None]), 0.0)
            total = lax.optimization_barrier(jnp.sum(weights, axis=2))
            weights_b = lax.optimization_barrier(weights.astype(jnp.bfloat16))
            numer = jnp.einsum('htk,khd->thd', weights_b.astype(jnp.float32), values.astype(jnp.float32))
            own = (numer / jnp.maximum(total, 1.0).T[:, :, None]).astype(jnp.bfloat16)
            own = lax.optimization_barrier(own)
            parts.append((own.astype(jnp.float32), top.T, total.T))
        best = parts[0][1]
        for part in parts[1:]:
            best = jnp.maximum(best, part[1])
        summed = jnp.zeros((SPAN, HEADS, HEAD_DIM), jnp.float32)
        denom = jnp.zeros((SPAN, HEADS), jnp.float32)
        for own, top, total in parts:
            share = total * jnp.exp(top - best)
            summed = summed + share[:, :, None] * own
            denom = denom + share
        attn = (summed / denom[:, :, None]).reshape(SPAN, D).astype(jnp.bfloat16)
        mixed = jnp.dot(attn, out_weight, preferred_element_type=jnp.float32) + out_bias + inputs.astype(jnp.float32)
        center = mixed - lax.optimization_barrier(jnp.mean(mixed, axis=1, keepdims=True))
        spread = lax.optimization_barrier(jnp.mean(center * center, axis=1, keepdims=True))
        return (center * lax.rsqrt(spread + 1e-05) * norm_gain + norm_bias).astype(jnp.bfloat16)
    return lax.map(one_slot, jnp.arange(REQUESTS))
```

```python
import functools

import jax
import jax.numpy as jnp
from jax import lax
from jax.experimental import pallas as pl
from jax.experimental.pallas import tpu as pltpu
from jax.sharding import PartitionSpec as P

HEAD_DIM = 64
LIVE = 3e38
DEAD = -1e30
F32 = jnp.float32
BF16 = jnp.bfloat16
MESH = pl.DeviceIdType.MESH


def peers():
    me = lax.axis_index("seq")
    core = me % 2
    partner = me + 1 - 2 * core
    twin = (me + 2) % 4
    diag = (partner + 2) % 4
    return me, core, partner, twin, diag


def greet(devices):
    barrier = pltpu.get_barrier_semaphore()
    for device in devices:
        pl.semaphore_signal(barrier, inc=1, device_id={"seq": device}, device_id_type=MESH)
    pl.semaphore_wait(barrier, len(devices))


def cols(index, width):
    return pl.ds(pl.multiple_of(index * width, 128), width)


def nt(a, b):
    return lax.dot_general(a, b, (((1,), (1,)), ((), ())), preferred_element_type=F32)


def attend(query, keys, caps, values, heads):
    rows, width = query.shape
    lane = lax.broadcasted_iota(jnp.int32, (rows, width), 1) // HEAD_DIM
    zero = jnp.zeros_like(query)
    stacked = jnp.concatenate([jnp.where(lane == h, query, zero) for h in range(heads)], 0)
    scores = [jnp.minimum(nt(stacked, k), cap) for k, cap in zip(keys, caps)]
    top = functools.reduce(jnp.maximum, [jnp.max(s, 1, keepdims=True) for s in scores])
    total, numer = 0.0, 0.0
    for s, v in zip(scores, values):
        weights = jnp.exp(s - top)
        total = total + jnp.sum(weights, 1, keepdims=True)
        numer = numer + jnp.dot(weights.astype(BF16), v, preferred_element_type=F32)
    return numer, top, total


def pick(stacked, rows, heads):
    width = heads * HEAD_DIM
    lane = lax.broadcasted_iota(jnp.int32, (rows, width), 1) // HEAD_DIM
    out = stacked[0:rows]
    for h in range(1, heads):
        out = jnp.where(lane == h, stacked[h * rows : (h + 1) * rows], out)
    return out


def stat_tile(top, total, rows, heads):
    lane = lax.broadcasted_iota(jnp.int32, (rows, 128), 1)
    out = jnp.ones((rows, 128), F32)
    for h in range(heads):
        out = jnp.where(lane == h, top[h * rows : (h + 1) * rows], out)
        out = jnp.where(lane == heads + h, total[h * rows : (h + 1) * rows], out)
    return out


def spread(tile, rows, heads):
    lane = lax.broadcasted_iota(jnp.int32, (rows, heads * HEAD_DIM), 1) // HEAD_DIM
    out = jnp.broadcast_to(tile[:, 0:1], (rows, heads * HEAD_DIM))
    for h in range(1, heads):
        out = jnp.where(lane == h, tile[:, h : h + 1], out)
    return out


def attention_kernel(
    cached_ref,
    span_ref,
    slot_ref,
    tokens_hbm,
    keys_hbm,
    values_hbm,
    weight_hbm,
    bias_ref,
    out_ref,
    tok,
    weight,
    kc,
    vc,
    kn,
    vn,
    qo,
    qt,
    numer_own,
    stat_own,
    part_send,
    part_recv,
    stat_send,
    stat_recv,
    attn,
    local_sem,
    tok_send,
    tok_recv,
    cache_send,
    cache_recv,
    q_send,
    q_recv,
    p_send,
    p_recv,
    a_send,
    a_recv,
):
    me, core, partner, twin, diag = peers()
    chip = me // 2
    rows = tok.shape[1]
    cache_rows = kc.shape[2]
    width = kc.shape[3]
    heads = width // HEAD_DIM
    request = slot_ref[lax.axis_index("dp")]
    cached = cached_ref[request]
    filled = span_ref[request]

    locals_ = [
        pltpu.make_async_copy(tokens_hbm.at[0], tok.at[me], local_sem.at[0]),
        pltpu.make_async_copy(weight_hbm, weight, local_sem.at[1]),
    ]
    for at, (hbm, buf) in enumerate(((keys_hbm, kc), (values_hbm, vc))):
        for group, owner in enumerate((me, twin)):
            locals_.append(
                pltpu.make_async_copy(
                    hbm.at[0, :, cols(owner, width)],
                    buf.at[group, core],
                    local_sem.at[2 + 2 * at + group],
                )
            )
    for copy in locals_:
        copy.start()

    greet((partner, twin))

    def remote(src, dst, send, recv, device):
        return pltpu.make_async_remote_copy(
            src_ref=src,
            dst_ref=dst,
            send_sem=send,
            recv_sem=recv,
            device_id={"seq": device},
            device_id_type=MESH,
        )

    to_twin = remote(tokens_hbm.at[0], tok.at[me], tok_send.at[1], tok_recv.at[1], twin)
    to_twin.start()
    to_partner = remote(tokens_hbm.at[0], tok.at[me], tok_send.at[0], tok_recv.at[0], partner)
    to_partner.start()
    forward = remote(tok.at[twin], tok.at[twin], tok_send.at[2], tok_recv.at[2], partner)
    cache_copies = []
    for at, (hbm, buf) in enumerate(((keys_hbm, kc), (values_hbm, vc))):
        for group, owner in enumerate((partner, diag)):
            cache_copies.append(
                remote(
                    hbm.at[0, :, cols(owner, width)],
                    buf.at[group, core],
                    cache_send.at[2 * at + group],
                    cache_recv.at[2 * at + group],
                    partner,
                )
            )
    for copy in cache_copies:
        copy.start()

    bias = bias_ref[:, cols(me, 3 * width)]
    low = lax.broadcasted_iota(jnp.int32, (rows, 128), 1) < HEAD_DIM

    def query_copy(block):
        return remote(qo.at[block], qt.at[block], q_send.at[block], q_recv.at[block], twin)

    def project(block):
        summed = jnp.dot(tok[block], weight[...], preferred_element_type=F32) + bias
        queries, keys, values = [], [], []
        for pair in range(heads // 2):
            a, b, c = (
                summed[:, (3 * pair + i) * 128 : (3 * pair + i + 1) * 128] for i in range(3)
            )
            queries.append(jnp.where(low, a, b))
            keys.append(pltpu.roll(jnp.where(low, c, a), HEAD_DIM, 1))
            values.append(jnp.where(low, b, c))
        scaled = jnp.concatenate(queries, 1).astype(BF16).astype(F32) * HEAD_DIM**-0.5
        qo[block] = scaled.astype(BF16)
        kn[block] = jnp.concatenate(keys, 1).astype(BF16)
        vn[block] = jnp.concatenate(values, 1).astype(BF16)
        query_copy(block).start()

    locals_[0].wait()
    locals_[1].wait()
    project(me)
    to_partner.wait_recv()
    project(partner)
    to_twin.wait_recv()
    forward.start()
    project(twin)
    forward.wait_recv()
    project(diag)

    for copy in locals_[2:]:
        copy.wait()
    for copy in cache_copies:
        copy.wait_recv()

    place = lax.broadcasted_iota(jnp.int32, (1, cache_rows), 1)
    caps = [
        jnp.where((2 * chip + j) * cache_rows + place < cached, LIVE, DEAD) for j in range(2)
    ]

    blocks = tok.shape[0]
    new_rows = blocks * rows
    for block in range(blocks):
        seen = (block + 1) * rows
        stacked_row = lax.broadcasted_iota(jnp.int32, (heads * rows, seen), 0) % rows
        new = lax.broadcasted_iota(jnp.int32, (heads * rows, seen), 1)
        alive = (new <= block * rows + stacked_row) & (new < filled)
        new_cap = jnp.where(alive, LIVE, DEAD)
        numer, top, total = attend(
            qo[block],
            [kc[0, 0], kc[0, 1], kn[0 : block + 1].reshape(seen, width)],
            caps + [new_cap],
            [vc[0, 0], vc[0, 1], vn[0 : block + 1].reshape(seen, width)],
            heads,
        )
        numer_own[block] = pick(numer, rows, heads)
        stat_own[block] = stat_tile(top, total, rows, heads)

    def part_copies(block):
        return (
            remote(
                part_send.at[block],
                part_recv.at[block],
                p_send.at[0, block],
                p_recv.at[0, block],
                twin,
            ),
            remote(
                stat_send.at[block],
                stat_recv.at[block],
                p_send.at[1, block],
                p_recv.at[1, block],
                twin,
            ),
        )

    def twin_block(block, carry):
        query_copy(block).wait_recv()
        numer, top, total = attend(
            qt[block], [kc[1, 0], kc[1, 1]], caps, [vc[1, 0], vc[1, 1]], heads
        )
        part_send[block] = pick(numer / total, rows, heads).astype(BF16)
        stat_send[block] = stat_tile(top, total, rows, heads).T[0 : 2 * heads]
        for copy in part_copies(block):
            copy.start()
        return carry

    lax.fori_loop(0, blocks, twin_block, 0)

    def combine(block, carry):
        for copy in part_copies(block):
            copy.wait_recv()
        other = jnp.concatenate(
            [stat_recv[block], jnp.ones((rows - 2 * heads, rows), F32)], 0
        ).T
        own = stat_own[block]
        best = jnp.maximum(own, other)
        scale_own = jnp.exp(own - best)
        scale_other = pltpu.roll(other, 128 - heads, 1) * jnp.exp(other - best)
        denom = pltpu.roll(own, 128 - heads, 1) * scale_own + scale_other
        mixed = numer_own[block] * spread(scale_own / denom, rows, heads)
        mixed = mixed + part_recv[block].astype(F32) * spread(scale_other / denom, rows, heads)
        attn[block] = mixed.astype(BF16)
        return carry

    lax.fori_loop(0, blocks, combine, 0)

    shared = [
        remote(attn.at[owner], out_ref.at[at, 1], a_send.at[at], a_recv.at[at], partner)
        for at, owner in enumerate((partner, diag))
    ]
    for copy in shared:
        copy.start()
    out_ref[0, 0] = attn[me]
    out_ref[1, 0] = attn[twin]
    for copy in shared:
        copy.wait()
    to_twin.wait_send()
    to_partner.wait_send()
    forward.wait_send()
    for copy in cache_copies:
        copy.wait_send()

    def drain(block, carry):
        query_copy(block).wait_send()
        for copy in part_copies(block):
            copy.wait_send()
        return carry

    lax.fori_loop(0, blocks, drain, 0)


def output_kernel(
    attn_ref, own_ref, other_ref, tokens_ref, bias_ref, gain_ref, shift_ref, out_ref, send, recv, s_sem, r_sem
):
    me, core, partner, twin, diag = peers()
    greet((twin,))

    def product(group):
        return jnp.dot(attn_ref[group, 0], own_ref[...], preferred_element_type=F32) + jnp.dot(
            attn_ref[group, 1], other_ref[...], preferred_element_type=F32
        )

    send[...] = product(1).astype(BF16)
    copy = pltpu.make_async_remote_copy(
        src_ref=send,
        dst_ref=recv,
        send_sem=s_sem,
        recv_sem=r_sem,
        device_id={"seq": twin},
        device_id_type=MESH,
    )
    copy.start()
    mixed = product(0) + bias_ref[...] + tokens_ref[0].astype(F32)
    copy.wait()
    mixed = mixed + recv[...].astype(F32)
    center = mixed - jnp.mean(mixed, axis=1, keepdims=True)
    variance = jnp.mean(center * center, axis=1, keepdims=True)
    normed = center * lax.rsqrt(variance + 1e-05) * gain_ref[...] + shift_ref[...]
    out_ref[0] = normed.astype(BF16)


def local(
    tokens,
    cache_keys,
    cache_values,
    qkv_weight,
    qkv_bias,
    out_weight,
    out_bias,
    norm_gain,
    norm_bias,
    cached_len,
    span_len,
    slot_request,
):
    rows, model = tokens.shape[1:]
    cache_rows = cache_keys.shape[1]
    width = qkv_weight.shape[1] // 3
    heads = width // HEAD_DIM
    blocks = lax.axis_size("seq")
    any_spec = pl.BlockSpec(memory_space=pl.ANY)
    vmem = pl.BlockSpec(memory_space=pltpu.VMEM)
    smem = pl.BlockSpec(memory_space=pltpu.SMEM)
    dma = pltpu.SemaphoreType.DMA

    own_weight = lax.all_gather(out_weight, "dp", axis=1, tiled=True)
    other_weight = lax.ppermute(own_weight, "seq", [(i, i ^ 1) for i in range(blocks)])

    attn = pl.pallas_call(
        attention_kernel,
        out_shape=jax.ShapeDtypeStruct((2, 2, rows, width), BF16),
        in_specs=[smem, smem, smem, any_spec, any_spec, any_spec, any_spec, vmem],
        out_specs=vmem,
        scratch_shapes=[
            pltpu.VMEM((blocks, rows, model), BF16),
            pltpu.VMEM((model, 3 * width), BF16),
            pltpu.VMEM((2, 2, cache_rows, width), BF16),
            pltpu.VMEM((2, 2, cache_rows, width), BF16),
            pltpu.VMEM((blocks, rows, width), BF16),
            pltpu.VMEM((blocks, rows, width), BF16),
            pltpu.VMEM((blocks, rows, width), BF16),
            pltpu.VMEM((blocks, rows, width), BF16),
            pltpu.VMEM((blocks, rows, width), F32),
            pltpu.VMEM((blocks, rows, 128), F32),
            pltpu.VMEM((blocks, rows, width), BF16),
            pltpu.VMEM((blocks, rows, width), BF16),
            pltpu.VMEM((blocks, 2 * heads, rows), F32),
            pltpu.VMEM((blocks, 2 * heads, rows), F32),
            pltpu.VMEM((blocks, rows, width), BF16),
            dma((6,)),
            dma((3,)),
            dma((3,)),
            dma((4,)),
            dma((4,)),
            dma((blocks,)),
            dma((blocks,)),
            dma((2, blocks)),
            dma((2, blocks)),
            dma((2,)),
            dma((2,)),
        ],
        compiler_params=pltpu.CompilerParams(
            collective_id=0, has_side_effects=True, vmem_limit_bytes=48 << 20
        ),
        cost_estimate=pl.CostEstimate(
            flops=6_000_000_000, bytes_accessed=6_000_000, transcendentals=5_000_000
        ),
        name="attention",
    )(
        cached_len,
        span_len,
        slot_request,
        tokens,
        cache_keys,
        cache_values,
        qkv_weight,
        qkv_bias.reshape(1, -1),
    )

    return pl.pallas_call(
        output_kernel,
        out_shape=jax.ShapeDtypeStruct((1, rows, model), BF16),
        in_specs=[vmem] * 7,
        out_specs=vmem,
        scratch_shapes=[
            pltpu.VMEM((rows, model), BF16),
            pltpu.VMEM((rows, model), BF16),
            dma,
            dma,
        ],
        compiler_params=pltpu.CompilerParams(
            collective_id=1, has_side_effects=True, vmem_limit_bytes=16 << 20
        ),
        cost_estimate=pl.CostEstimate(
            flops=300_000_000, bytes_accessed=2_000_000, transcendentals=0
        ),
        name="output",
    )(
        attn,
        own_weight,
        other_weight,
        tokens,
        out_bias.reshape(1, -1),
        norm_gain.reshape(1, -1),
        norm_bias.reshape(1, -1),
    )


def solution(mesh):
    return jax.shard_map(
        local,
        mesh=mesh,
        in_specs=(
            P("dp", "seq", None),
            P("dp", "seq", None),
            P("dp", "seq", None),
            P(None, "seq"),
            P(),
            P("seq", "dp"),
            P(),
            P(),
            P(),
            P(),
            P(),
            P(),
        ),
        out_specs=P("dp", "seq", None),
        check_vma=False,
    )
```

```python
import functools

import jax
import jax.numpy as jnp
from jax import lax
from jax.experimental import pallas as pl
from jax.experimental.pallas import tpu as pltpu
from jax.sharding import PartitionSpec as P

HEAD_DIM = 64
LIVE = 3e38
DEAD = -1e30
F32 = jnp.float32
BF16 = jnp.bfloat16
MESH = pl.DeviceIdType.MESH


def peers():
    me = lax.axis_index("seq")
    core = me % 2
    partner = me + 1 - 2 * core
    twin = (me + 2) % 4
    diag = (partner + 2) % 4
    return me, core, partner, twin, diag


def cols(index, width):
    return pl.ds(pl.multiple_of(index * width, 128), width)


def nt(a, b):
    return lax.dot_general(a, b, (((1,), (1,)), ((), ())), preferred_element_type=F32)


def attend(query, keys, caps, values, heads):
    rows, width = query.shape
    lane = lax.broadcasted_iota(jnp.int32, (rows, width), 1) // HEAD_DIM
    zero = jnp.zeros_like(query)
    stacked = jnp.concatenate([jnp.where(lane == h, query, zero) for h in range(heads)], 0)
    scores = [jnp.minimum(nt(stacked, k), cap) for k, cap in zip(keys, caps)]
    top = functools.reduce(jnp.maximum, [jnp.max(s, 1, keepdims=True) for s in scores])
    total, numer = 0.0, 0.0
    for s, v in zip(scores, values):
        weights = jnp.exp(s - top)
        total = total + jnp.sum(weights, 1, keepdims=True)
        numer = numer + jnp.dot(weights.astype(BF16), v, preferred_element_type=F32)
    return numer, top, total


def pick(stacked, rows, heads):
    width = heads * HEAD_DIM
    lane = lax.broadcasted_iota(jnp.int32, (rows, width), 1) // HEAD_DIM
    out = stacked[0:rows]
    for h in range(1, heads):
        out = jnp.where(lane == h, stacked[h * rows : (h + 1) * rows], out)
    return out


def stat_tile(top, total, rows, heads):
    lane = lax.broadcasted_iota(jnp.int32, (rows, 128), 1)
    out = jnp.ones((rows, 128), F32)
    for h in range(heads):
        out = jnp.where(lane == h, top[h * rows : (h + 1) * rows], out)
        out = jnp.where(lane == heads + h, total[h * rows : (h + 1) * rows], out)
    return out


def spread(tile, rows, heads):
    lane = lax.broadcasted_iota(jnp.int32, (rows, heads * HEAD_DIM), 1) // HEAD_DIM
    out = jnp.broadcast_to(tile[:, 0:1], (rows, heads * HEAD_DIM))
    for h in range(1, heads):
        out = jnp.where(lane == h, tile[:, h : h + 1], out)
    return out


def kernel(
    gather,
    cached_ref,
    span_ref,
    slot_ref,
    tokens_hbm,
    keys_hbm,
    values_hbm,
    weight_hbm,
    out_weight_hbm,
    bias_ref,
    out_bias_ref,
    gain_ref,
    shift_ref,
    out_ref,
    tok,
    weight,
    kc,
    vc,
    kn,
    vn,
    qo,
    qt,
    numer_own,
    stat_own,
    part_send,
    part_recv,
    stat_send,
    stat_recv,
    attn,
    other_attn,
    wo,
    other_wo,
    y_send,
    y_recv,
    local_sem,
    tok_send,
    tok_recv,
    cache_send,
    cache_recv,
    q_send,
    q_recv,
    p_send,
    p_recv,
    a_send,
    a_recv,
    w_send,
    w_recv,
    f_sem,
    ys_sem,
    yr_sem,
):
    me, core, partner, twin, diag = peers()
    chip = me // 2
    rows = tok.shape[1]
    cache_rows = kc.shape[2]
    width = kc.shape[3]
    heads = width // HEAD_DIM
    request = slot_ref[lax.axis_index("dp")]
    cached = cached_ref[request]
    filled = span_ref[request]

    locals_ = [
        pltpu.make_async_copy(tokens_hbm.at[0], tok.at[me], local_sem.at[0]),
        pltpu.make_async_copy(weight_hbm, weight, local_sem.at[1]),
    ]
    for at, (hbm, buf) in enumerate(((keys_hbm, kc), (values_hbm, vc))):
        for group, owner in enumerate((me, twin)):
            locals_.append(
                pltpu.make_async_copy(
                    hbm.at[0, :, cols(owner, width)],
                    buf.at[group, core],
                    local_sem.at[2 + 2 * at + group],
                )
            )
    dp = lax.axis_index("dp")
    parts = lax.axis_size("dp")
    if gather:
        piece = out_weight_hbm.shape[1]
        mine = wo.at[:, cols(dp, piece)]
    else:
        mine = wo
    own_weight = pltpu.make_async_copy(out_weight_hbm, mine, local_sem.at[6])
    for copy in locals_:
        copy.start()
    own_weight.start()

    barrier = pltpu.get_barrier_semaphore()
    near = [{"seq": partner}, {"seq": twin}]
    far = [{"dp": (dp + k) % parts} for k in range(1, parts)] if gather else []
    for device in near + far:
        pl.semaphore_signal(barrier, inc=1, device_id=device, device_id_type=MESH)
    pl.semaphore_wait(barrier, len(near + far))

    def remote(src, dst, send, recv, device):
        return pltpu.make_async_remote_copy(
            src_ref=src,
            dst_ref=dst,
            send_sem=send,
            recv_sem=recv,
            device_id={"seq": device},
            device_id_type=MESH,
        )

    to_twin = remote(tokens_hbm.at[0], tok.at[me], tok_send.at[1], tok_recv.at[1], twin)
    to_twin.start()
    to_partner = remote(tokens_hbm.at[0], tok.at[me], tok_send.at[0], tok_recv.at[0], partner)
    to_partner.start()
    forward = remote(tok.at[twin], tok.at[twin], tok_send.at[2], tok_recv.at[2], partner)
    cache_copies = []
    for at, (hbm, buf) in enumerate(((keys_hbm, kc), (values_hbm, vc))):
        for group, owner in enumerate((partner, diag)):
            cache_copies.append(
                remote(
                    hbm.at[0, :, cols(owner, width)],
                    buf.at[group, core],
                    cache_send.at[2 * at + group],
                    cache_recv.at[2 * at + group],
                    partner,
                )
            )
    for copy in cache_copies:
        copy.start()
    weight_copies = [
        pltpu.make_async_remote_copy(
            src_ref=out_weight_hbm,
            dst_ref=mine,
            send_sem=w_send.at[k],
            recv_sem=w_recv.at[k],
            device_id=device,
            device_id_type=MESH,
        )
        for k, device in enumerate(far)
    ]
    for copy in weight_copies:
        copy.start()

    bias = bias_ref[:, cols(me, 3 * width)]
    low = lax.broadcasted_iota(jnp.int32, (rows, 128), 1) < HEAD_DIM

    def query_copy(block):
        return remote(qo.at[block], qt.at[block], q_send.at[block], q_recv.at[block], twin)

    def project(block):
        summed = jnp.dot(tok[block], weight[...], preferred_element_type=F32) + bias
        queries, keys, values = [], [], []
        for pair in range(heads // 2):
            a, b, c = (
                summed[:, (3 * pair + i) * 128 : (3 * pair + i + 1) * 128] for i in range(3)
            )
            queries.append(jnp.where(low, a, b))
            keys.append(pltpu.roll(jnp.where(low, c, a), HEAD_DIM, 1))
            values.append(jnp.where(low, b, c))
        scaled = jnp.concatenate(queries, 1).astype(BF16).astype(F32) * HEAD_DIM**-0.5
        qo[block] = scaled.astype(BF16)
        kn[block] = jnp.concatenate(keys, 1).astype(BF16)
        vn[block] = jnp.concatenate(values, 1).astype(BF16)
        query_copy(block).start()

    locals_[0].wait()
    locals_[1].wait()
    project(me)
    to_partner.wait_recv()
    project(partner)
    to_twin.wait_recv()
    forward.start()
    project(twin)
    forward.wait_recv()
    project(diag)

    for copy in locals_[2:]:
        copy.wait()
    for copy in cache_copies:
        copy.wait_recv()

    place = lax.broadcasted_iota(jnp.int32, (1, cache_rows), 1)
    caps = [
        jnp.where((2 * chip + j) * cache_rows + place < cached, LIVE, DEAD) for j in range(2)
    ]

    blocks = tok.shape[0]
    new_rows = blocks * rows
    for block in range(blocks):
        seen = (block + 1) * rows
        stacked_row = lax.broadcasted_iota(jnp.int32, (heads * rows, seen), 0) % rows
        new = lax.broadcasted_iota(jnp.int32, (heads * rows, seen), 1)
        alive = (new <= block * rows + stacked_row) & (new < filled)
        new_cap = jnp.where(alive, LIVE, DEAD)
        numer, top, total = attend(
            qo[block],
            [kc[0, 0], kc[0, 1], kn[0 : block + 1].reshape(seen, width)],
            caps + [new_cap],
            [vc[0, 0], vc[0, 1], vn[0 : block + 1].reshape(seen, width)],
            heads,
        )
        numer_own[block] = pick(numer, rows, heads)
        stat_own[block] = stat_tile(top, total, rows, heads)

    own_weight.wait()
    for copy in weight_copies:
        copy.wait_recv()
    share_weight = remote(wo, other_wo, f_sem.at[0], f_sem.at[1], partner)
    share_weight.start()

    def part_copies(block):
        return (
            remote(
                part_send.at[block],
                part_recv.at[block],
                p_send.at[0, block],
                p_recv.at[0, block],
                twin,
            ),
            remote(
                stat_send.at[block],
                stat_recv.at[block],
                p_send.at[1, block],
                p_recv.at[1, block],
                twin,
            ),
        )

    def twin_block(step, carry):
        block = 2 * ((chip + step // 2) % 2) + (core + step // 2 + step + 1) % 2
        query_copy(block).wait_recv()
        numer, top, total = attend(
            qt[block], [kc[1, 0], kc[1, 1]], caps, [vc[1, 0], vc[1, 1]], heads
        )
        part_send[block] = pick(numer / total, rows, heads).astype(BF16)
        stat_send[block] = stat_tile(top, total, rows, heads).T[0 : 2 * heads]
        for copy in part_copies(block):
            copy.start()
        return carry

    def combine(block):
        for copy in part_copies(block):
            copy.wait_recv()
        other = jnp.concatenate(
            [stat_recv[block], jnp.ones((rows - 2 * heads, rows), F32)], 0
        ).T
        own = stat_own[block]
        best = jnp.maximum(own, other)
        scale_own = jnp.exp(own - best)
        scale_other = pltpu.roll(other, 128 - heads, 1) * jnp.exp(other - best)
        denom = pltpu.roll(own, 128 - heads, 1) * scale_own + scale_other
        mixed = numer_own[block] * spread(scale_own / denom, rows, heads)
        mixed = mixed + part_recv[block].astype(F32) * spread(scale_other / denom, rows, heads)
        attn[block] = mixed.astype(BF16)

    shared = [
        remote(attn.at[owner], other_attn.at[at], a_send.at[at], a_recv.at[at], partner)
        for at, owner in enumerate((partner, diag))
    ]
    pieces, _, span = y_send.shape

    def product(block, at, piece):
        here = slice(piece * span, (piece + 1) * span)
        return jnp.dot(attn[block], wo[:, here], preferred_element_type=F32) + jnp.dot(
            other_attn[at], other_wo[:, here], preferred_element_type=F32
        )

    y_copies = [
        remote(y_send.at[i], y_recv.at[i], ys_sem.at[i], yr_sem.at[i], twin)
        for i in range(pieces)
    ]

    lax.fori_loop(0, blocks - 1, twin_block, 0)
    combine(diag)
    shared[1].start()
    combine(twin)
    twin_block(blocks - 1, 0)
    share_weight.wait_recv()
    shared[1].wait_recv()
    for i in range(pieces):
        y_send[i] = product(twin, 1, i).astype(BF16)
        y_copies[i].start()
    combine(partner)
    shared[0].start()
    combine(me)
    shared[0].wait_recv()
    mixed = [product(me, 0, i) for i in range(pieces)]
    for i in range(pieces):
        y_copies[i].wait_recv()
    mixed = jnp.concatenate(
        [mixed[i] + y_recv[i].astype(F32) for i in range(pieces)], 1
    )
    mixed = mixed + out_bias_ref[...] + tok[me].astype(F32)
    center = mixed - jnp.mean(mixed, axis=1, keepdims=True)
    variance = jnp.mean(center * center, axis=1, keepdims=True)
    normed = center * lax.rsqrt(variance + 1e-05) * gain_ref[...] + shift_ref[...]
    out_ref[0] = normed.astype(BF16)

    for copy in [to_twin, to_partner, forward, share_weight]:
        copy.wait_send()
    for copy in cache_copies + weight_copies + shared + y_copies:
        copy.wait_send()

    def drain(block, carry):
        query_copy(block).wait_send()
        for copy in part_copies(block):
            copy.wait_send()
        return carry

    lax.fori_loop(0, blocks, drain, 0)


def local(
    tokens,
    cache_keys,
    cache_values,
    qkv_weight,
    qkv_bias,
    out_weight,
    out_bias,
    norm_gain,
    norm_bias,
    cached_len,
    span_len,
    slot_request,
):
    rows, model = tokens.shape[1:]
    cache_rows = cache_keys.shape[1]
    width = qkv_weight.shape[1] // 3
    heads = width // HEAD_DIM
    blocks = lax.axis_size("seq")
    hbm = pl.BlockSpec(memory_space=pltpu.HBM)
    vmem = pl.BlockSpec(memory_space=pltpu.VMEM)
    smem = pl.BlockSpec(memory_space=pltpu.SMEM)
    dma = pltpu.SemaphoreType.DMA

    gather = out_weight.shape[1] % 128 == 0
    if not gather:
        out_weight = lax.all_gather(out_weight, "dp", axis=1, tiled=True)
    far = lax.axis_size("dp") - 1 if gather else 1
    pieces = 4

    def half(count):
        return pltpu.VMEM((count, rows, width), BF16)

    return pl.pallas_call(
        functools.partial(kernel, gather),
        out_shape=jax.ShapeDtypeStruct((1, rows, model), BF16),
        in_specs=[smem] * 3 + [hbm] * 5 + [vmem] * 4,
        out_specs=vmem,
        scratch_shapes=[
            pltpu.VMEM((blocks, rows, model), BF16),
            pltpu.VMEM((model, 3 * width), BF16),
            pltpu.VMEM((2, 2, cache_rows, width), BF16),
            pltpu.VMEM((2, 2, cache_rows, width), BF16),
            half(blocks),
            half(blocks),
            half(blocks),
            half(blocks),
            pltpu.VMEM((blocks, rows, width), F32),
            pltpu.VMEM((blocks, rows, 128), F32),
            half(blocks),
            half(blocks),
            pltpu.VMEM((blocks, 2 * heads, rows), F32),
            pltpu.VMEM((blocks, 2 * heads, rows), F32),
            half(blocks),
            half(2),
            pltpu.VMEM((width, model), BF16),
            pltpu.VMEM((width, model), BF16),
            pltpu.VMEM((pieces, rows, model // pieces), BF16),
            pltpu.VMEM((pieces, rows, model // pieces), BF16),
            dma((7,)),
            dma((3,)),
            dma((3,)),
            dma((4,)),
            dma((4,)),
            dma((blocks,)),
            dma((blocks,)),
            dma((2, blocks)),
            dma((2, blocks)),
            dma((2,)),
            dma((2,)),
            dma((far,)),
            dma((far,)),
            dma((2,)),
            dma((pieces,)),
            dma((pieces,)),
        ],
        compiler_params=pltpu.CompilerParams(
            collective_id=0, has_side_effects=True, vmem_limit_bytes=60 << 20
        ),
        cost_estimate=pl.CostEstimate(
            flops=6_000_000_000, bytes_accessed=6_000_000, transcendentals=5_000_000
        ),
        name="sublayer",
    )(
        cached_len,
        span_len,
        slot_request,
        tokens,
        cache_keys,
        cache_values,
        qkv_weight,
        out_weight,
        qkv_bias.reshape(1, -1),
        out_bias.reshape(1, -1),
        norm_gain.reshape(1, -1),
        norm_bias.reshape(1, -1),
    )


def solution(mesh):
    return jax.shard_map(
        local,
        mesh=mesh,
        in_specs=(
            P("dp", "seq", None),
            P("dp", "seq", None),
            P("dp", "seq", None),
            P(None, "seq"),
            P(),
            P("seq", "dp"),
            P(),
            P(),
            P(),
            P(),
            P(),
            P(),
        ),
        out_specs=P("dp", "seq", None),
        check_vma=False,
    )
```

```python
import functools

import jax
import jax.numpy as jnp
from jax import lax
from jax.experimental import pallas as pl
from jax.experimental.pallas import tpu as pltpu
from jax.sharding import PartitionSpec as P

HEAD_DIM = 64
LIVE = 3e38
DEAD = -1e30
F32 = jnp.float32
BF16 = jnp.bfloat16
MESH = pl.DeviceIdType.MESH


def peers():
    me = lax.axis_index("seq")
    core = me % 2
    partner = me + 1 - 2 * core
    twin = (me + 2) % 4
    diag = (partner + 2) % 4
    return me, core, partner, twin, diag


def cols(index, width):
    return pl.ds(pl.multiple_of(index * width, 128), width)


def nt(a, b):
    return lax.dot_general(a, b, (((1,), (1,)), ((), ())), preferred_element_type=F32)


def attend(query, keys, caps, values, heads):
    rows, width = query.shape
    lane = lax.broadcasted_iota(jnp.int32, (rows, width), 1) // HEAD_DIM
    zero = jnp.zeros_like(query)
    stacked = jnp.concatenate([jnp.where(lane == h, query, zero) for h in range(heads)], 0)
    scores = [jnp.minimum(nt(stacked, k), cap) for k, cap in zip(keys, caps)]
    top = functools.reduce(jnp.maximum, [jnp.max(s, 1, keepdims=True) for s in scores])
    total, numer = 0.0, 0.0
    for s, v in zip(scores, values):
        weights = jnp.exp(s - top)
        total = total + jnp.sum(weights, 1, keepdims=True)
        numer = numer + jnp.dot(weights.astype(BF16), v, preferred_element_type=F32)
    return numer, top, total


def pick(stacked, rows, heads):
    width = heads * HEAD_DIM
    lane = lax.broadcasted_iota(jnp.int32, (rows, width), 1) // HEAD_DIM
    out = stacked[0:rows]
    for h in range(1, heads):
        out = jnp.where(lane == h, stacked[h * rows : (h + 1) * rows], out)
    return out


def stat_tile(top, total, rows, heads):
    lane = lax.broadcasted_iota(jnp.int32, (rows, 128), 1)
    out = jnp.ones((rows, 128), F32)
    for h in range(heads):
        out = jnp.where(lane == h, top[h * rows : (h + 1) * rows], out)
        out = jnp.where(lane == heads + h, total[h * rows : (h + 1) * rows], out)
    return out


def spread(tile, rows, heads):
    lane = lax.broadcasted_iota(jnp.int32, (rows, heads * HEAD_DIM), 1) // HEAD_DIM
    out = jnp.broadcast_to(tile[:, 0:1], (rows, heads * HEAD_DIM))
    for h in range(1, heads):
        out = jnp.where(lane == h, tile[:, h : h + 1], out)
    return out


def kernel(
    gather,
    cached_ref,
    span_ref,
    slot_ref,
    tokens_hbm,
    keys_hbm,
    values_hbm,
    weight_hbm,
    out_weight_hbm,
    bias_ref,
    out_bias_ref,
    gain_ref,
    shift_ref,
    out_ref,
    tok,
    weight,
    kc,
    vc,
    kn,
    vn,
    qo,
    qt,
    numer_keep,
    stat_keep,
    part_send,
    part_recv,
    stat_send,
    stat_recv,
    attn,
    other_attn,
    wo,
    local_sem,
    tok_send,
    tok_recv,
    cache_send,
    cache_recv,
    q_send,
    q_recv,
    p_send,
    p_recv,
    a_send,
    a_recv,
    w_send,
    w_recv,
    f_sem,
    g_sem,
):
    me, core, partner, twin, diag = peers()
    chip = me // 2
    rows = tok.shape[1]
    cache_rows = kc.shape[2]
    width = kc.shape[3]
    heads = width // HEAD_DIM
    request = slot_ref[lax.axis_index("dp")]
    cached = cached_ref[request]
    filled = span_ref[request]

    locals_ = [
        pltpu.make_async_copy(tokens_hbm.at[0], tok.at[me], local_sem.at[0]),
        pltpu.make_async_copy(weight_hbm, weight, local_sem.at[1]),
    ]
    for at, (hbm, buf) in enumerate(((keys_hbm, kc), (values_hbm, vc))):
        for group, owner in enumerate((me, twin)):
            locals_.append(
                pltpu.make_async_copy(
                    hbm.at[0, :, cols(owner, width)],
                    buf.at[group, core],
                    local_sem.at[2 + 2 * at + group],
                )
            )
    dp = lax.axis_index("dp")
    parts = lax.axis_size("dp")
    if gather:
        piece = out_weight_hbm.shape[1]
        mine = wo.at[me, :, cols(dp, piece)]
        theirs = wo.at[twin, :, cols(dp, piece)]
    else:
        mine = wo
    own_weight = pltpu.make_async_copy(out_weight_hbm, mine, local_sem.at[6])
    for copy in locals_:
        copy.start()
    own_weight.start()

    barrier = pltpu.get_barrier_semaphore()
    near = [{"seq": partner}, {"seq": twin}]
    far = [{"dp": (dp + k) % parts} for k in range(1, parts)] if gather else []
    for device in near + far:
        pl.semaphore_signal(barrier, inc=1, device_id=device, device_id_type=MESH)
    pl.semaphore_wait(barrier, len(near + far))

    def remote(src, dst, send, recv, device):
        return pltpu.make_async_remote_copy(
            src_ref=src,
            dst_ref=dst,
            send_sem=send,
            recv_sem=recv,
            device_id={"seq": device},
            device_id_type=MESH,
        )

    to_twin = remote(tokens_hbm.at[0], tok.at[me], tok_send.at[1], tok_recv.at[1], twin)
    to_twin.start()
    to_partner = remote(tokens_hbm.at[0], tok.at[me], tok_send.at[0], tok_recv.at[0], partner)
    to_partner.start()
    forward = remote(tok.at[twin], tok.at[twin], tok_send.at[2], tok_recv.at[2], partner)
    cache_copies = []
    for at, (hbm, buf) in enumerate(((keys_hbm, kc), (values_hbm, vc))):
        for group, owner in enumerate((partner, diag)):
            cache_copies.append(
                remote(
                    hbm.at[0, :, cols(owner, width)],
                    buf.at[group, core],
                    cache_send.at[2 * at + group],
                    cache_recv.at[2 * at + group],
                    partner,
                )
            )
    for copy in cache_copies:
        copy.start()
    weight_copies = [
        pltpu.make_async_remote_copy(
            src_ref=out_weight_hbm,
            dst_ref=mine,
            send_sem=w_send.at[k],
            recv_sem=w_recv.at[k],
            device_id=device,
            device_id_type=MESH,
        )
        for k, device in enumerate(far)
    ]
    for copy in weight_copies:
        copy.start()
    if gather:
        weight_twin = remote(out_weight_hbm, mine, g_sem.at[0], g_sem.at[1], twin)
        weight_forward = [
            pltpu.make_async_remote_copy(
                src_ref=theirs,
                dst_ref=theirs,
                send_sem=w_send.at[len(far) + k],
                recv_sem=w_recv.at[len(far) + k],
                device_id=device,
                device_id_type=MESH,
            )
            for k, device in enumerate(far)
        ]

    bias = bias_ref[:, cols(me, 3 * width)]
    low = lax.broadcasted_iota(jnp.int32, (rows, 128), 1) < HEAD_DIM

    def query_copy(block):
        return remote(qo.at[block], qt.at[block], q_send.at[block], q_recv.at[block], twin)

    def project(block):
        summed = jnp.dot(tok[block], weight[...], preferred_element_type=F32) + bias
        queries, keys, values = [], [], []
        for pair in range(heads // 2):
            a, b, c = (
                summed[:, (3 * pair + i) * 128 : (3 * pair + i + 1) * 128] for i in range(3)
            )
            queries.append(jnp.where(low, a, b))
            keys.append(pltpu.roll(jnp.where(low, c, a), HEAD_DIM, 1))
            values.append(jnp.where(low, b, c))
        scaled = jnp.concatenate(queries, 1).astype(BF16).astype(F32) * HEAD_DIM**-0.5
        qo[block] = scaled.astype(BF16)
        kn[block] = jnp.concatenate(keys, 1).astype(BF16)
        vn[block] = jnp.concatenate(values, 1).astype(BF16)
        query_copy(block).start()

    locals_[0].wait()
    locals_[1].wait()
    project(me)
    to_partner.wait_recv()
    project(partner)
    to_twin.wait_send()
    if gather:
        weight_twin.start()
    to_twin.wait_recv()
    forward.start()
    project(twin)
    forward.wait_recv()
    project(diag)

    for copy in locals_[2:]:
        copy.wait()
    for copy in cache_copies:
        copy.wait_recv()

    place = lax.broadcasted_iota(jnp.int32, (1, cache_rows), 1)
    caps = [
        jnp.where((2 * chip + j) * cache_rows + place < cached, LIVE, DEAD) for j in range(2)
    ]

    blocks = tok.shape[0]
    new_rows = blocks * rows
    new = lax.broadcasted_iota(jnp.int32, (heads * rows, new_rows), 1)
    stacked_row = lax.broadcasted_iota(jnp.int32, (heads * rows, new_rows), 0) % rows

    def part_copies(group, slot):
        return (
            remote(
                part_send.at[group, slot],
                part_recv.at[1 - group, slot],
                p_send.at[0, group, slot],
                p_recv.at[0, 1 - group, slot],
                twin,
            ),
            remote(
                stat_send.at[group, slot],
                stat_recv.at[1 - group, slot],
                p_send.at[1, group, slot],
                p_recv.at[1, 1 - group, slot],
                twin,
            ),
        )

    def partial(group, local_rows):
        def body(slot, carry):
            base = chip if local_rows else 1 - chip
            block = 2 * base + (core + slot) % 2
            if group == 0:
                alive = (new <= block * rows + stacked_row) & (new < filled)
                numer, top, total = attend(
                    qo[block],
                    [kc[0, 0], kc[0, 1], kn[...].reshape(new_rows, width)],
                    caps + [jnp.where(alive, LIVE, DEAD)],
                    [vc[0, 0], vc[0, 1], vn[...].reshape(new_rows, width)],
                    heads,
                )
            else:
                query_copy(block).wait_recv()
                numer, top, total = attend(
                    qt[block], [kc[1, 0], kc[1, 1]], caps, [vc[1, 0], vc[1, 1]], heads
                )
            stats = stat_tile(top, total, rows, heads)
            if local_rows:
                numer_keep[group, slot] = pick(numer, rows, heads)
                stat_keep[group, slot] = stats
            else:
                part_send[group, slot] = pick(numer / total, rows, heads).astype(BF16)
                stat_send[group, slot] = stats.T[0 : 2 * heads]
                for copy in part_copies(group, slot):
                    copy.start()
            return carry

        lax.fori_loop(0, 2, body, 0)

    def combine(group, slot):
        for copy in part_copies(1 - group, slot):
            copy.wait_recv()
        other = jnp.concatenate(
            [stat_recv[group, slot], jnp.ones((rows - 2 * heads, rows), F32)], 0
        ).T
        own = stat_keep[group, slot]
        best = jnp.maximum(own, other)
        scale_own = pltpu.roll(own, 128 - heads, 1) * jnp.exp(own - best)
        scale_other = pltpu.roll(other, 128 - heads, 1) * jnp.exp(other - best)
        denom = scale_own + scale_other
        first = jnp.exp(own - best) / denom
        mixed = numer_keep[group, slot] * spread(first, rows, heads)
        mixed = mixed + part_recv[group, slot].astype(F32) * spread(
            scale_other / denom, rows, heads
        )
        attn[slot, group] = mixed.astype(BF16)

    partial(0, False)
    if gather:
        weight_twin.wait_recv()
        for copy in weight_forward:
            copy.start()
    partial(1, False)
    partial(0, True)
    partial(1, True)

    own_weight.wait()
    for copy in weight_copies:
        copy.wait_recv()
    late = []
    if gather:
        for copy in weight_forward:
            copy.wait_recv()
        late = [
            remote(wo.at[owner], wo.at[owner], f_sem.at[0, at], f_sem.at[1, at], partner)
            for at, owner in enumerate((me, twin))
        ]
    for copy in late:
        copy.start()

    shared = remote(attn.at[1], other_attn, a_send.at[0], a_recv.at[0], partner)
    combine(0, 1)
    combine(1, 1)
    shared.start()
    combine(0, 0)
    combine(1, 0)
    mixed = jnp.dot(attn[0, 0], wo[me], preferred_element_type=F32)
    mixed = mixed + jnp.dot(attn[0, 1], wo[twin], preferred_element_type=F32)
    for copy in late:
        copy.wait_recv()
    shared.wait_recv()
    mixed = mixed + jnp.dot(other_attn[0], wo[partner], preferred_element_type=F32)
    mixed = mixed + jnp.dot(other_attn[1], wo[diag], preferred_element_type=F32)
    mixed = mixed + out_bias_ref[...] + tok[me].astype(F32)
    center = mixed - jnp.mean(mixed, axis=1, keepdims=True)
    variance = jnp.mean(center * center, axis=1, keepdims=True)
    normed = center * lax.rsqrt(variance + 1e-05) * gain_ref[...] + shift_ref[...]
    out_ref[0] = normed.astype(BF16)

    late.append(shared)
    if gather:
        late.append(weight_twin)
        late.extend(weight_forward)
    for copy in [to_partner, forward] + late + cache_copies + weight_copies:
        copy.wait_send()

    def drain(block, carry):
        query_copy(block).wait_send()
        return carry

    lax.fori_loop(0, blocks, drain, 0)
    for group in range(2):
        for slot in range(2):
            for copy in part_copies(group, slot):
                copy.wait_send()


def local(
    tokens,
    cache_keys,
    cache_values,
    qkv_weight,
    qkv_bias,
    out_weight,
    out_bias,
    norm_gain,
    norm_bias,
    cached_len,
    span_len,
    slot_request,
):
    rows, model = tokens.shape[1:]
    cache_rows = cache_keys.shape[1]
    width = qkv_weight.shape[1] // 3
    heads = width // HEAD_DIM
    blocks = lax.axis_size("seq")
    hbm = pl.BlockSpec(memory_space=pltpu.HBM)
    vmem = pl.BlockSpec(memory_space=pltpu.VMEM)
    smem = pl.BlockSpec(memory_space=pltpu.SMEM)
    dma = pltpu.SemaphoreType.DMA

    gather = out_weight.shape[1] % 128 == 0
    if not gather:
        out_weight = lax.all_gather(out_weight, "dp", axis=1, tiled=True)
        out_weight = lax.all_gather(out_weight, "seq", axis=0)
    far = lax.axis_size("dp") - 1 if gather else 1

    def half(count):
        return pltpu.VMEM((count, rows, width), BF16)

    return pl.pallas_call(
        functools.partial(kernel, gather),
        out_shape=jax.ShapeDtypeStruct((1, rows, model), BF16),
        in_specs=[smem] * 3 + [hbm] * 5 + [vmem] * 4,
        out_specs=vmem,
        scratch_shapes=[
            pltpu.VMEM((blocks, rows, model), BF16),
            pltpu.VMEM((model, 3 * width), BF16),
            pltpu.VMEM((2, 2, cache_rows, width), BF16),
            pltpu.VMEM((2, 2, cache_rows, width), BF16),
            half(blocks),
            half(blocks),
            half(blocks),
            half(blocks),
            pltpu.VMEM((2, 2, rows, width), F32),
            pltpu.VMEM((2, 2, rows, 128), F32),
            pltpu.VMEM((2, 2, rows, width), BF16),
            pltpu.VMEM((2, 2, rows, width), BF16),
            pltpu.VMEM((2, 2, 2 * heads, rows), F32),
            pltpu.VMEM((2, 2, 2 * heads, rows), F32),
            pltpu.VMEM((2, 2, rows, width), BF16),
            half(2),
            pltpu.VMEM((blocks, width, model), BF16),
            dma((7,)),
            dma((3,)),
            dma((3,)),
            dma((4,)),
            dma((4,)),
            dma((blocks,)),
            dma((blocks,)),
            dma((2, 2, 2)),
            dma((2, 2, 2)),
            dma((1,)),
            dma((1,)),
            dma((2 * far,)),
            dma((2 * far,)),
            dma((2, 2)),
            dma((2,)),
        ],
        compiler_params=pltpu.CompilerParams(
            collective_id=0, has_side_effects=True, vmem_limit_bytes=60 << 20
        ),
        cost_estimate=pl.CostEstimate(
            flops=6_000_000_000, bytes_accessed=6_000_000, transcendentals=5_000_000
        ),
        name="sublayer",
    )(
        cached_len,
        span_len,
        slot_request,
        tokens,
        cache_keys,
        cache_values,
        qkv_weight,
        out_weight,
        qkv_bias.reshape(1, -1),
        out_bias.reshape(1, -1),
        norm_gain.reshape(1, -1),
        norm_bias.reshape(1, -1),
    )


def solution(mesh):
    return jax.shard_map(
        local,
        mesh=mesh,
        in_specs=(
            P("dp", "seq", None),
            P("dp", "seq", None),
            P("dp", "seq", None),
            P(None, "seq"),
            P(),
            P("seq", "dp"),
            P(),
            P(),
            P(),
            P(),
            P(),
            P(),
        ),
        out_specs=P("dp", "seq", None),
        check_vma=False,
    )
```

```python
import functools

import jax
import jax.numpy as jnp
from jax import lax
from jax.experimental import pallas as pl
from jax.experimental.pallas import tpu as pltpu
from jax.sharding import PartitionSpec as P

HEAD_DIM = 64
LIVE = 3e38
DEAD = -1e30
F32 = jnp.float32
BF16 = jnp.bfloat16
MESH = pl.DeviceIdType.MESH


def peers():
    me = lax.axis_index("seq")
    core = me % 2
    partner = me + 1 - 2 * core
    twin = (me + 2) % 4
    diag = (partner + 2) % 4
    return me, core, partner, twin, diag


def cols(index, width):
    return pl.ds(pl.multiple_of(index * width, 128), width)


def nt(a, b):
    return lax.dot_general(a, b, (((1,), (1,)), ((), ())), preferred_element_type=F32)


def attend(query, keys, caps, values, heads, before=None):
    rows, width = query.shape
    lane = lax.broadcasted_iota(jnp.int32, (rows, width), 1) // HEAD_DIM
    zero = jnp.zeros_like(query)
    stacked = jnp.concatenate([jnp.where(lane == h, query, zero) for h in range(heads)], 0)
    scores = [jnp.minimum(nt(stacked, k), cap) for k, cap in zip(keys, caps)]
    top = functools.reduce(jnp.maximum, [jnp.max(s, 1, keepdims=True) for s in scores])
    total, numer = 0.0, 0.0
    if before is not None:
        top = jnp.maximum(top, before[1])
        fade = jnp.exp(before[1] - top)
        numer, total = before[0] * fade, before[2] * fade
    for s, v in zip(scores, values):
        weights = jnp.exp(s - top)
        total = total + jnp.sum(weights, 1, keepdims=True)
        numer = numer + jnp.dot(weights.astype(BF16), v, preferred_element_type=F32)
    return numer, top, total


def pick(stacked, rows, heads):
    width = heads * HEAD_DIM
    lane = lax.broadcasted_iota(jnp.int32, (rows, width), 1) // HEAD_DIM
    out = stacked[0:rows]
    for h in range(1, heads):
        out = jnp.where(lane == h, stacked[h * rows : (h + 1) * rows], out)
    return out


def stat_tile(top, total, rows, heads):
    lane = lax.broadcasted_iota(jnp.int32, (rows, 128), 1)
    out = jnp.ones((rows, 128), F32)
    for h in range(heads):
        out = jnp.where(lane == h, top[h * rows : (h + 1) * rows], out)
        out = jnp.where(lane == heads + h, total[h * rows : (h + 1) * rows], out)
    return out


def spread(tile, rows, heads):
    lane = lax.broadcasted_iota(jnp.int32, (rows, heads * HEAD_DIM), 1) // HEAD_DIM
    out = jnp.broadcast_to(tile[:, 0:1], (rows, heads * HEAD_DIM))
    for h in range(1, heads):
        out = jnp.where(lane == h, tile[:, h : h + 1], out)
    return out


def kernel(
    gather,
    cached_ref,
    span_ref,
    slot_ref,
    tokens_hbm,
    keys_hbm,
    values_hbm,
    weight_hbm,
    out_weight_hbm,
    bias_ref,
    out_bias_ref,
    gain_ref,
    shift_ref,
    out_ref,
    tok,
    weight,
    kc,
    vc,
    kn,
    vn,
    qo,
    qt,
    numer_keep,
    stat_keep,
    early_numer,
    early_stat,
    part_send,
    part_recv,
    stat_send,
    stat_recv,
    attn,
    other_attn,
    wo,
    local_sem,
    tok_send,
    tok_recv,
    cache_send,
    cache_recv,
    q_send,
    q_recv,
    p_send,
    p_recv,
    a_send,
    a_recv,
    w_send,
    w_recv,
    f_sem,
    g_sem,
):
    me, core, partner, twin, diag = peers()
    chip = me // 2
    rows = tok.shape[1]
    cache_rows = kc.shape[2]
    width = kc.shape[3]
    heads = width // HEAD_DIM
    request = slot_ref[lax.axis_index("dp")]
    cached = cached_ref[request]
    filled = span_ref[request]

    locals_ = [
        pltpu.make_async_copy(tokens_hbm.at[0], tok.at[me], local_sem.at[0]),
        pltpu.make_async_copy(weight_hbm, weight, local_sem.at[1]),
    ]
    for at, (hbm, buf) in enumerate(((keys_hbm, kc), (values_hbm, vc))):
        for group, owner in enumerate((me, twin)):
            locals_.append(
                pltpu.make_async_copy(
                    hbm.at[0, :, cols(owner, width)],
                    buf.at[group, core],
                    local_sem.at[2 + 2 * at + group],
                )
            )
    dp = lax.axis_index("dp")
    parts = lax.axis_size("dp")
    if gather:
        piece = out_weight_hbm.shape[1]
        mine = wo.at[me, :, cols(dp, piece)]
        theirs = wo.at[twin, :, cols(dp, piece)]
    else:
        mine = wo
    own_weight = pltpu.make_async_copy(out_weight_hbm, mine, local_sem.at[6])
    for copy in locals_:
        copy.start()
    own_weight.start()

    barrier = pltpu.get_barrier_semaphore()
    near = [{"seq": partner}, {"seq": twin}]
    far = [{"dp": (dp + k) % parts} for k in range(1, parts)] if gather else []
    for device in near + far:
        pl.semaphore_signal(barrier, inc=1, device_id=device, device_id_type=MESH)
    pl.semaphore_wait(barrier, len(near + far))

    def remote(src, dst, send, recv, device):
        return pltpu.make_async_remote_copy(
            src_ref=src,
            dst_ref=dst,
            send_sem=send,
            recv_sem=recv,
            device_id={"seq": device},
            device_id_type=MESH,
        )

    to_twin = remote(tokens_hbm.at[0], tok.at[me], tok_send.at[1], tok_recv.at[1], twin)
    to_twin.start()
    to_partner = remote(tokens_hbm.at[0], tok.at[me], tok_send.at[0], tok_recv.at[0], partner)
    to_partner.start()
    forward = remote(tok.at[twin], tok.at[twin], tok_send.at[2], tok_recv.at[2], partner)
    cache_copies = []
    for at, (hbm, buf) in enumerate(((keys_hbm, kc), (values_hbm, vc))):
        for group, owner in enumerate((partner, diag)):
            cache_copies.append(
                remote(
                    hbm.at[0, :, cols(owner, width)],
                    buf.at[group, core],
                    cache_send.at[2 * at + group],
                    cache_recv.at[2 * at + group],
                    partner,
                )
            )
    for copy in cache_copies:
        copy.start()
    weight_copies = [
        pltpu.make_async_remote_copy(
            src_ref=out_weight_hbm,
            dst_ref=mine,
            send_sem=w_send.at[k],
            recv_sem=w_recv.at[k],
            device_id=device,
            device_id_type=MESH,
        )
        for k, device in enumerate(far)
    ]
    for copy in weight_copies:
        copy.start()
    if gather:
        weight_twin = remote(out_weight_hbm, mine, g_sem.at[0], g_sem.at[1], twin)
        weight_forward = [
            pltpu.make_async_remote_copy(
                src_ref=theirs,
                dst_ref=theirs,
                send_sem=w_send.at[len(far) + k],
                recv_sem=w_recv.at[len(far) + k],
                device_id=device,
                device_id_type=MESH,
            )
            for k, device in enumerate(far)
        ]

    bias = bias_ref[:, cols(me, 3 * width)]
    low = lax.broadcasted_iota(jnp.int32, (rows, 128), 1) < HEAD_DIM

    def query_copy(block):
        return remote(qo.at[block], qt.at[block], q_send.at[block], q_recv.at[block], twin)

    def project(block):
        summed = jnp.dot(tok[block], weight[...], preferred_element_type=F32) + bias
        queries, keys, values = [], [], []
        for pair in range(heads // 2):
            a, b, c = (
                summed[:, (3 * pair + i) * 128 : (3 * pair + i + 1) * 128] for i in range(3)
            )
            queries.append(jnp.where(low, a, b))
            keys.append(pltpu.roll(jnp.where(low, c, a), HEAD_DIM, 1))
            values.append(jnp.where(low, b, c))
        scaled = jnp.concatenate(queries, 1).astype(BF16).astype(F32) * HEAD_DIM**-0.5
        qo[block] = scaled.astype(BF16)
        kn[block] = jnp.concatenate(keys, 1).astype(BF16)
        vn[block] = jnp.concatenate(values, 1).astype(BF16)
        query_copy(block).start()

    locals_[0].wait()
    locals_[1].wait()
    project(me)
    to_partner.wait_recv()
    project(partner)
    to_twin.wait_send()
    if gather:
        weight_twin.start()

    for copy in locals_[2:]:
        copy.wait()
    for copy in cache_copies:
        copy.wait_recv()
    place = lax.broadcasted_iota(jnp.int32, (1, cache_rows), 1)
    caps = [
        jnp.where((2 * chip + j) * cache_rows + place < cached, LIVE, DEAD) for j in range(2)
    ]

    def early(slot, carry):
        block = 2 * chip + (core + slot) % 2
        numer, top, total = attend(
            qo[block], [kc[0, 0], kc[0, 1]], caps, [vc[0, 0], vc[0, 1]], heads
        )
        early_numer[slot] = numer
        early_stat[slot, 0] = top
        early_stat[slot, 1] = total
        return carry

    lax.fori_loop(0, 2, early, 0)
    to_twin.wait_recv()
    forward.start()
    project(twin)
    forward.wait_recv()
    project(diag)

    blocks = tok.shape[0]
    new_rows = blocks * rows
    new = lax.broadcasted_iota(jnp.int32, (heads * rows, new_rows), 1)
    stacked_row = lax.broadcasted_iota(jnp.int32, (heads * rows, new_rows), 0) % rows

    def part_copies(group, slot):
        return (
            remote(
                part_send.at[group, slot],
                part_recv.at[1 - group, slot],
                p_send.at[0, group, slot],
                p_recv.at[0, 1 - group, slot],
                twin,
            ),
            remote(
                stat_send.at[group, slot],
                stat_recv.at[1 - group, slot],
                p_send.at[1, group, slot],
                p_recv.at[1, 1 - group, slot],
                twin,
            ),
        )

    def partial(group, local_rows):
        def body(slot, carry):
            base = chip if local_rows else 1 - chip
            block = 2 * base + (core + slot) % 2
            if group == 0:
                alive = (new <= block * rows + stacked_row) & (new < filled)
                keys = [kn[...].reshape(new_rows, width)]
                values = [vn[...].reshape(new_rows, width)]
                limits = [jnp.where(alive, LIVE, DEAD)]
                before = None
                if local_rows:
                    before = (early_numer[slot], early_stat[slot, 0], early_stat[slot, 1])
                else:
                    keys = [kc[0, 0], kc[0, 1]] + keys
                    values = [vc[0, 0], vc[0, 1]] + values
                    limits = caps + limits
                numer, top, total = attend(qo[block], keys, limits, values, heads, before)
            else:
                query_copy(block).wait_recv()
                numer, top, total = attend(
                    qt[block], [kc[1, 0], kc[1, 1]], caps, [vc[1, 0], vc[1, 1]], heads
                )
            stats = stat_tile(top, total, rows, heads)
            if local_rows:
                numer_keep[group, slot] = pick(numer, rows, heads)
                stat_keep[group, slot] = stats
            else:
                part_send[group, slot] = pick(numer * (1.0 / total), rows, heads).astype(BF16)
                stat_send[group, slot] = stats.T[0 : 2 * heads]
                for copy in part_copies(group, slot):
                    copy.start()
            return carry

        lax.fori_loop(0, 2, body, 0)

    def combine(group, slot):
        for copy in part_copies(1 - group, slot):
            copy.wait_recv()
        other = jnp.concatenate(
            [stat_recv[group, slot], jnp.ones((rows - 2 * heads, rows), F32)], 0
        ).T
        own = stat_keep[group, slot]
        best = jnp.maximum(own, other)
        scale_own = pltpu.roll(own, 128 - heads, 1) * jnp.exp(own - best)
        scale_other = pltpu.roll(other, 128 - heads, 1) * jnp.exp(other - best)
        denom = scale_own + scale_other
        first = jnp.exp(own - best) / denom
        mixed = numer_keep[group, slot] * spread(first, rows, heads)
        mixed = mixed + part_recv[group, slot].astype(F32) * spread(
            scale_other / denom, rows, heads
        )
        attn[slot, group] = mixed.astype(BF16)

    partial(0, False)
    if gather:
        weight_twin.wait_recv()
        for copy in weight_forward:
            copy.start()
    partial(1, False)
    partial(0, True)
    partial(1, True)

    own_weight.wait()
    for copy in weight_copies:
        copy.wait_recv()
    late = []
    if gather:
        for copy in weight_forward:
            copy.wait_recv()
        late = [
            remote(wo.at[owner], wo.at[owner], f_sem.at[0, at], f_sem.at[1, at], partner)
            for at, owner in enumerate((me, twin))
        ]
    for copy in late:
        copy.start()

    shared = remote(attn.at[1], other_attn, a_send.at[0], a_recv.at[0], partner)
    combine(0, 1)
    combine(1, 1)
    shared.start()
    combine(0, 0)
    combine(1, 0)
    mixed = jnp.dot(attn[0, 0], wo[me], preferred_element_type=F32)
    mixed = mixed + jnp.dot(attn[0, 1], wo[twin], preferred_element_type=F32)
    for copy in late:
        copy.wait_recv()
    shared.wait_recv()
    mixed = mixed + jnp.dot(other_attn[0], wo[partner], preferred_element_type=F32)
    mixed = mixed + jnp.dot(other_attn[1], wo[diag], preferred_element_type=F32)
    mixed = mixed + out_bias_ref[...] + tok[me].astype(F32)
    center = mixed - jnp.mean(mixed, axis=1, keepdims=True)
    variance = jnp.mean(center * center, axis=1, keepdims=True)
    normed = center * lax.rsqrt(variance + 1e-05) * gain_ref[...] + shift_ref[...]
    out_ref[0] = normed.astype(BF16)

    late.append(shared)
    if gather:
        late.append(weight_twin)
        late.extend(weight_forward)
    for copy in [to_partner, forward] + late + cache_copies + weight_copies:
        copy.wait_send()

    def drain(block, carry):
        query_copy(block).wait_send()
        return carry

    lax.fori_loop(0, blocks, drain, 0)
    for group in range(2):
        for slot in range(2):
            for copy in part_copies(group, slot):
                copy.wait_send()


def local(
    tokens,
    cache_keys,
    cache_values,
    qkv_weight,
    qkv_bias,
    out_weight,
    out_bias,
    norm_gain,
    norm_bias,
    cached_len,
    span_len,
    slot_request,
):
    rows, model = tokens.shape[1:]
    cache_rows = cache_keys.shape[1]
    width = qkv_weight.shape[1] // 3
    heads = width // HEAD_DIM
    blocks = lax.axis_size("seq")
    hbm = pl.BlockSpec(memory_space=pltpu.HBM)
    vmem = pl.BlockSpec(memory_space=pltpu.VMEM)
    smem = pl.BlockSpec(memory_space=pltpu.SMEM)
    dma = pltpu.SemaphoreType.DMA

    gather = out_weight.shape[1] % 128 == 0
    if not gather:
        out_weight = lax.all_gather(out_weight, "dp", axis=1, tiled=True)
        out_weight = lax.all_gather(out_weight, "seq", axis=0)
    far = lax.axis_size("dp") - 1 if gather else 1

    def half(count):
        return pltpu.VMEM((count, rows, width), BF16)

    return pl.pallas_call(
        functools.partial(kernel, gather),
        out_shape=jax.ShapeDtypeStruct((1, rows, model), BF16),
        in_specs=[smem] * 3 + [hbm] * 5 + [vmem] * 4,
        out_specs=vmem,
        scratch_shapes=[
            pltpu.VMEM((blocks, rows, model), BF16),
            pltpu.VMEM((model, 3 * width), BF16),
            pltpu.VMEM((2, 2, cache_rows, width), BF16),
            pltpu.VMEM((2, 2, cache_rows, width), BF16),
            half(blocks),
            half(blocks),
            half(blocks),
            half(blocks),
            pltpu.VMEM((2, 2, rows, width), F32),
            pltpu.VMEM((2, 2, rows, 128), F32),
            pltpu.VMEM((2, heads * rows, width), F32),
            pltpu.VMEM((2, 2, heads * rows, 1), F32),
            pltpu.VMEM((2, 2, rows, width), BF16),
            pltpu.VMEM((2, 2, rows, width), BF16),
            pltpu.VMEM((2, 2, 2 * heads, rows), F32),
            pltpu.VMEM((2, 2, 2 * heads, rows), F32),
            pltpu.VMEM((2, 2, rows, width), BF16),
            half(2),
            pltpu.VMEM((blocks, width, model), BF16),
            dma((7,)),
            dma((3,)),
            dma((3,)),
            dma((4,)),
            dma((4,)),
            dma((blocks,)),
            dma((blocks,)),
            dma((2, 2, 2)),
            dma((2, 2, 2)),
            dma((1,)),
            dma((1,)),
            dma((2 * far,)),
            dma((2 * far,)),
            dma((2, 2)),
            dma((2,)),
        ],
        compiler_params=pltpu.CompilerParams(
            collective_id=0, has_side_effects=True, vmem_limit_bytes=60 << 20
        ),
        cost_estimate=pl.CostEstimate(
            flops=6_000_000_000, bytes_accessed=6_000_000, transcendentals=5_000_000
        ),
        name="sublayer",
    )(
        cached_len,
        span_len,
        slot_request,
        tokens,
        cache_keys,
        cache_values,
        qkv_weight,
        out_weight,
        qkv_bias.reshape(1, -1),
        out_bias.reshape(1, -1),
        norm_gain.reshape(1, -1),
        norm_bias.reshape(1, -1),
    )


def solution(mesh):
    return jax.shard_map(
        local,
        mesh=mesh,
        in_specs=(
            P("dp", "seq", None),
            P("dp", "seq", None),
            P("dp", "seq", None),
            P(None, "seq"),
            P(),
            P("seq", "dp"),
            P(),
            P(),
            P(),
            P(),
            P(),
            P(),
        ),
        out_specs=P("dp", "seq", None),
        check_vma=False,
    )
```

```python
import functools

import jax
import jax.numpy as jnp
from jax import lax
from jax.experimental import pallas as pl
from jax.experimental.pallas import tpu as pltpu
from jax.sharding import PartitionSpec as P

HEAD_DIM = 64
LIVE = 3e38
DEAD = -1e30
F32 = jnp.float32
BF16 = jnp.bfloat16
MESH = pl.DeviceIdType.MESH


def peers():
    me = lax.axis_index("seq")
    core = me % 2
    partner = me + 1 - 2 * core
    twin = (me + 2) % 4
    diag = (partner + 2) % 4
    return me, core, partner, twin, diag


def cols(index, width):
    return pl.ds(pl.multiple_of(index * width, 128), width)


def nt(a, b):
    return lax.dot_general(a, b, (((1,), (1,)), ((), ())), preferred_element_type=F32)


def attend(query, keys, caps, values, heads):
    rows, width = query.shape
    lane = lax.broadcasted_iota(jnp.int32, (rows, width), 1) // HEAD_DIM
    zero = jnp.zeros_like(query)
    stacked = jnp.concatenate([jnp.where(lane == h, query, zero) for h in range(heads)], 0)
    scores = [jnp.minimum(nt(stacked, k), cap) for k, cap in zip(keys, caps)]
    top = functools.reduce(jnp.maximum, [jnp.max(s, 1, keepdims=True) for s in scores])
    total, numer = 0.0, 0.0
    for s, v in zip(scores, values):
        weights = jnp.exp(s - top)
        total = total + jnp.sum(weights, 1, keepdims=True)
        numer = numer + jnp.dot(weights.astype(BF16), v, preferred_element_type=F32)
    return numer, top, total


def pick(stacked, rows, heads):
    width = heads * HEAD_DIM
    lane = lax.broadcasted_iota(jnp.int32, (rows, width), 1) // HEAD_DIM
    out = stacked[0:rows]
    for h in range(1, heads):
        out = jnp.where(lane == h, stacked[h * rows : (h + 1) * rows], out)
    return out


def stat_tile(top, total, rows, heads):
    lane = lax.broadcasted_iota(jnp.int32, (rows, 128), 1)
    out = jnp.ones((rows, 128), F32)
    for h in range(heads):
        out = jnp.where(lane == h, top[h * rows : (h + 1) * rows], out)
        out = jnp.where(lane == heads + h, total[h * rows : (h + 1) * rows], out)
    return out


def spread(tile, rows, heads):
    lane = lax.broadcasted_iota(jnp.int32, (rows, heads * HEAD_DIM), 1) // HEAD_DIM
    out = jnp.broadcast_to(tile[:, 0:1], (rows, heads * HEAD_DIM))
    for h in range(1, heads):
        out = jnp.where(lane == h, tile[:, h : h + 1], out)
    return out


def kernel(
    gather,
    cached_ref,
    span_ref,
    slot_ref,
    tokens_hbm,
    keys_hbm,
    values_hbm,
    weight_hbm,
    out_weight_hbm,
    bias_ref,
    out_bias_ref,
    gain_ref,
    shift_ref,
    out_ref,
    tok,
    weight,
    kc,
    vc,
    kn,
    vn,
    qo,
    qt,
    numer_keep,
    stat_keep,
    part_send,
    part_recv,
    stat_send,
    stat_recv,
    attn,
    other_attn,
    wo,
    local_sem,
    tok_send,
    tok_recv,
    cache_send,
    cache_recv,
    q_send,
    q_recv,
    p_send,
    p_recv,
    a_send,
    a_recv,
    w_send,
    w_recv,
    f_sem,
    g_sem,
):
    me, core, partner, twin, diag = peers()
    chip = me // 2
    rows = tok.shape[1]
    cache_rows = kc.shape[2]
    width = kc.shape[3]
    heads = width // HEAD_DIM
    request = slot_ref[lax.axis_index("dp")]
    cached = cached_ref[request]
    filled = span_ref[request]

    locals_ = [
        pltpu.make_async_copy(tokens_hbm.at[0], tok.at[me], local_sem.at[0]),
        pltpu.make_async_copy(weight_hbm, weight, local_sem.at[1]),
    ]
    for at, (hbm, buf) in enumerate(((keys_hbm, kc), (values_hbm, vc))):
        for group, owner in enumerate((me, twin)):
            locals_.append(
                pltpu.make_async_copy(
                    hbm.at[0, :, cols(owner, width)],
                    buf.at[group, core],
                    local_sem.at[2 + 2 * at + group],
                )
            )
    dp = lax.axis_index("dp")
    parts = lax.axis_size("dp")
    if gather:
        piece = out_weight_hbm.shape[1]
        mine = wo.at[me, :, cols(dp, piece)]
        theirs = wo.at[twin, :, cols(dp, piece)]
    else:
        mine = wo
    own_weight = pltpu.make_async_copy(out_weight_hbm, mine, local_sem.at[6])
    for copy in locals_:
        copy.start()
    own_weight.start()

    barrier = pltpu.get_barrier_semaphore()
    near = [{"seq": partner}, {"seq": twin}]
    far = [{"dp": (dp + k) % parts} for k in range(1, parts)] if gather else []
    for device in near + far:
        pl.semaphore_signal(barrier, inc=1, device_id=device, device_id_type=MESH)
    pl.semaphore_wait(barrier, len(near + far))

    def remote(src, dst, send, recv, device):
        return pltpu.make_async_remote_copy(
            src_ref=src,
            dst_ref=dst,
            send_sem=send,
            recv_sem=recv,
            device_id={"seq": device},
            device_id_type=MESH,
        )

    to_twin = remote(tokens_hbm.at[0], tok.at[me], tok_send.at[1], tok_recv.at[1], twin)
    to_twin.start()
    to_partner = remote(tokens_hbm.at[0], tok.at[me], tok_send.at[0], tok_recv.at[0], partner)
    to_partner.start()
    forward = remote(tok.at[twin], tok.at[twin], tok_send.at[2], tok_recv.at[2], partner)
    cache_copies = []
    for at, (hbm, buf) in enumerate(((keys_hbm, kc), (values_hbm, vc))):
        for group, owner in enumerate((partner, diag)):
            cache_copies.append(
                remote(
                    hbm.at[0, :, cols(owner, width)],
                    buf.at[group, core],
                    cache_send.at[2 * at + group],
                    cache_recv.at[2 * at + group],
                    partner,
                )
            )
    for copy in cache_copies:
        copy.start()
    weight_copies = [
        pltpu.make_async_remote_copy(
            src_ref=out_weight_hbm,
            dst_ref=mine,
            send_sem=w_send.at[k],
            recv_sem=w_recv.at[k],
            device_id=device,
            device_id_type=MESH,
        )
        for k, device in enumerate(far)
    ]
    for copy in weight_copies:
        copy.start()
    if gather:
        weight_twin = remote(out_weight_hbm, mine, g_sem.at[0], g_sem.at[1], twin)
        weight_forward = [
            pltpu.make_async_remote_copy(
                src_ref=theirs,
                dst_ref=theirs,
                send_sem=w_send.at[len(far) + k],
                recv_sem=w_recv.at[len(far) + k],
                device_id=device,
                device_id_type=MESH,
            )
            for k, device in enumerate(far)
        ]

    bias = bias_ref[:, cols(me, 3 * width)]
    low = lax.broadcasted_iota(jnp.int32, (rows, 128), 1) < HEAD_DIM

    def query_copy(block):
        return remote(qo.at[block], qt.at[block], q_send.at[block], q_recv.at[block], twin)

    def project(block):
        summed = jnp.dot(tok[block], weight[...], preferred_element_type=F32) + bias
        queries, keys, values = [], [], []
        for pair in range(heads // 2):
            a, b, c = (
                summed[:, (3 * pair + i) * 128 : (3 * pair + i + 1) * 128] for i in range(3)
            )
            queries.append(jnp.where(low, a, b))
            keys.append(pltpu.roll(jnp.where(low, c, a), HEAD_DIM, 1))
            values.append(jnp.where(low, b, c))
        scaled = jnp.concatenate(queries, 1).astype(BF16).astype(F32) * HEAD_DIM**-0.5
        qo[block] = scaled.astype(BF16)
        kn[block] = jnp.concatenate(keys, 1).astype(BF16)
        vn[block] = jnp.concatenate(values, 1).astype(BF16)
        query_copy(block).start()

    locals_[0].wait()
    locals_[1].wait()
    project(me)
    to_partner.wait_recv()
    project(partner)
    to_twin.wait_send()
    if gather:
        weight_twin.start()
    to_twin.wait_recv()
    forward.start()
    project(twin)
    forward.wait_recv()
    project(diag)

    for copy in locals_[2:]:
        copy.wait()
    for copy in cache_copies:
        copy.wait_recv()

    place = lax.broadcasted_iota(jnp.int32, (1, cache_rows), 1)
    caps = [
        jnp.where((2 * chip + j) * cache_rows + place < cached, LIVE, DEAD) for j in range(2)
    ]

    blocks = tok.shape[0]
    new_rows = blocks * rows
    new = lax.broadcasted_iota(jnp.int32, (heads * rows, new_rows), 1)
    stacked_row = lax.broadcasted_iota(jnp.int32, (heads * rows, new_rows), 0) % rows
    ahead = jnp.where(new < filled, new - stacked_row, 2 * new_rows)

    def part_copies(group, slot):
        return (
            remote(
                part_send.at[group, slot],
                part_recv.at[1 - group, slot],
                p_send.at[0, group, slot],
                p_recv.at[0, 1 - group, slot],
                twin,
            ),
            remote(
                stat_send.at[group, slot],
                stat_recv.at[1 - group, slot],
                p_send.at[1, group, slot],
                p_recv.at[1, 1 - group, slot],
                twin,
            ),
        )

    def partial(group, local_rows):
        def body(slot, carry):
            base = chip if local_rows else 1 - chip
            block = 2 * base + (core + slot) % 2
            if group == 0:
                alive = ahead <= block * rows
                numer, top, total = attend(
                    qo[block],
                    [kc[0, 0], kc[0, 1], kn[...].reshape(new_rows, width)],
                    caps + [jnp.where(alive, LIVE, DEAD)],
                    [vc[0, 0], vc[0, 1], vn[...].reshape(new_rows, width)],
                    heads,
                )
            else:
                query_copy(block).wait_recv()
                numer, top, total = attend(
                    qt[block], [kc[1, 0], kc[1, 1]], caps, [vc[1, 0], vc[1, 1]], heads
                )
            stats = stat_tile(top, total, rows, heads)
            if local_rows:
                numer_keep[group, slot] = pick(numer, rows, heads)
                stat_keep[group, slot] = stats
            else:
                part_send[group, slot] = pick(numer * (1.0 / total), rows, heads).astype(BF16)
                stat_send[group, slot] = stats.T[0 : 2 * heads]
                for copy in part_copies(group, slot):
                    copy.start()
            return carry

        lax.fori_loop(0, 2, body, 0)

    def combine(group, slot):
        for copy in part_copies(1 - group, slot):
            copy.wait_recv()
        other = jnp.concatenate(
            [stat_recv[group, slot], jnp.ones((rows - 2 * heads, rows), F32)], 0
        ).T
        own = stat_keep[group, slot]
        best = jnp.maximum(own, other)
        scale_own = pltpu.roll(own, 128 - heads, 1) * jnp.exp(own - best)
        scale_other = pltpu.roll(other, 128 - heads, 1) * jnp.exp(other - best)
        denom = scale_own + scale_other
        first = jnp.exp(own - best) / denom
        mixed = numer_keep[group, slot] * spread(first, rows, heads)
        mixed = mixed + part_recv[group, slot].astype(F32) * spread(
            scale_other / denom, rows, heads
        )
        attn[slot, group] = mixed.astype(BF16)

    partial(0, False)
    if gather:
        weight_twin.wait_recv()
        for copy in weight_forward:
            copy.start()
    partial(1, False)
    partial(0, True)
    partial(1, True)

    own_weight.wait()
    for copy in weight_copies:
        copy.wait_recv()
    late = []
    if gather:
        for copy in weight_forward:
            copy.wait_recv()
        late = [
            remote(wo.at[owner], wo.at[owner], f_sem.at[0, at], f_sem.at[1, at], partner)
            for at, owner in enumerate((me, twin))
        ]
    for copy in late:
        copy.start()

    shared = remote(attn.at[1], other_attn, a_send.at[0], a_recv.at[0], partner)
    combine(0, 1)
    combine(1, 1)
    shared.start()
    combine(0, 0)
    combine(1, 0)
    mixed = jnp.dot(attn[0, 0], wo[me], preferred_element_type=F32)
    mixed = mixed + jnp.dot(attn[0, 1], wo[twin], preferred_element_type=F32)
    for copy in late:
        copy.wait_recv()
    shared.wait_recv()
    mixed = mixed + jnp.dot(other_attn[0], wo[partner], preferred_element_type=F32)
    mixed = mixed + jnp.dot(other_attn[1], wo[diag], preferred_element_type=F32)
    mixed = mixed + out_bias_ref[...] + tok[me].astype(F32)
    center = mixed - jnp.mean(mixed, axis=1, keepdims=True)
    variance = jnp.mean(center * center, axis=1, keepdims=True)
    normed = center * lax.rsqrt(variance + 1e-05) * gain_ref[...] + shift_ref[...]
    out_ref[0] = normed.astype(BF16)

    late.append(shared)
    if gather:
        late.append(weight_twin)
        late.extend(weight_forward)
    for copy in [to_partner, forward] + late + cache_copies + weight_copies:
        copy.wait_send()

    def drain(block, carry):
        query_copy(block).wait_send()
        return carry

    lax.fori_loop(0, blocks, drain, 0)
    for group in range(2):
        for slot in range(2):
            for copy in part_copies(group, slot):
                copy.wait_send()


def local(
    tokens,
    cache_keys,
    cache_values,
    qkv_weight,
    qkv_bias,
    out_weight,
    out_bias,
    norm_gain,
    norm_bias,
    cached_len,
    span_len,
    slot_request,
):
    rows, model = tokens.shape[1:]
    cache_rows = cache_keys.shape[1]
    width = qkv_weight.shape[1] // 3
    heads = width // HEAD_DIM
    blocks = lax.axis_size("seq")
    hbm = pl.BlockSpec(memory_space=pltpu.HBM)
    vmem = pl.BlockSpec(memory_space=pltpu.VMEM)
    smem = pl.BlockSpec(memory_space=pltpu.SMEM)
    dma = pltpu.SemaphoreType.DMA

    gather = out_weight.shape[1] % 128 == 0
    if not gather:
        out_weight = lax.all_gather(out_weight, "dp", axis=1, tiled=True)
        out_weight = lax.all_gather(out_weight, "seq", axis=0)
    far = lax.axis_size("dp") - 1 if gather else 1

    def half(count):
        return pltpu.VMEM((count, rows, width), BF16)

    return pl.pallas_call(
        functools.partial(kernel, gather),
        out_shape=jax.ShapeDtypeStruct((1, rows, model), BF16),
        in_specs=[smem] * 3 + [hbm] * 5 + [vmem] * 4,
        out_specs=vmem,
        scratch_shapes=[
            pltpu.VMEM((blocks, rows, model), BF16),
            pltpu.VMEM((model, 3 * width), BF16),
            pltpu.VMEM((2, 2, cache_rows, width), BF16),
            pltpu.VMEM((2, 2, cache_rows, width), BF16),
            half(blocks),
            half(blocks),
            half(blocks),
            half(blocks),
            pltpu.VMEM((2, 2, rows, width), F32),
            pltpu.VMEM((2, 2, rows, 128), F32),
            pltpu.VMEM((2, 2, rows, width), BF16),
            pltpu.VMEM((2, 2, rows, width), BF16),
            pltpu.VMEM((2, 2, 2 * heads, rows), F32),
            pltpu.VMEM((2, 2, 2 * heads, rows), F32),
            pltpu.VMEM((2, 2, rows, width), BF16),
            half(2),
            pltpu.VMEM((blocks, width, model), BF16),
            dma((7,)),
            dma((3,)),
            dma((3,)),
            dma((4,)),
            dma((4,)),
            dma((blocks,)),
            dma((blocks,)),
            dma((2, 2, 2)),
            dma((2, 2, 2)),
            dma((1,)),
            dma((1,)),
            dma((2 * far,)),
            dma((2 * far,)),
            dma((2, 2)),
            dma((2,)),
        ],
        compiler_params=pltpu.CompilerParams(
            collective_id=0, has_side_effects=True, vmem_limit_bytes=60 << 20
        ),
        cost_estimate=pl.CostEstimate(
            flops=6_000_000_000, bytes_accessed=6_000_000, transcendentals=5_000_000
        ),
        name="sublayer",
    )(
        cached_len,
        span_len,
        slot_request,
        tokens,
        cache_keys,
        cache_values,
        qkv_weight,
        out_weight,
        qkv_bias.reshape(1, -1),
        out_bias.reshape(1, -1),
        norm_gain.reshape(1, -1),
        norm_bias.reshape(1, -1),
    )


def solution(mesh):
    return jax.shard_map(
        local,
        mesh=mesh,
        in_specs=(
            P("dp", "seq", None),
            P("dp", "seq", None),
            P("dp", "seq", None),
            P(None, "seq"),
            P(),
            P("seq", "dp"),
            P(),
            P(),
            P(),
            P(),
            P(),
            P(),
        ),
        out_specs=P("dp", "seq", None),
        check_vma=False,
    )
```
